32 devices in a mesh: ctx: 2 (over y), exp: 16 (over z, x, core).
Axes of the slice: x: 2, y: 2, z: 4, core: 2. Of those that a mesh axis runs over, the one named last changes fastest.
Arguments:
- residual: bfloat16 [16, 128, 2048], P('exp', 'ctx'), may hold values from -1 to 1
- queries: bfloat16 [16, 128, 2048], P('exp', 'ctx'), may hold values from -6 to 6
- key_rows: bfloat16 [16, 128, 256], P('exp', 'ctx'), may hold values from -6 to 6
- value_rows: bfloat16 [16, 128, 256], P('exp', 'ctx'), may hold values from -0.8984375 to 0.8984375
- span_order: int32 [4], replicated, may hold values from 0 to 3, as said below
- norm_gain: float32 [2048], replicated, may hold values from 0.1 to 1.9
- gate_logits: float32 [16, 128, 8], P('exp', 'ctx'), may hold values from -6 to 6
- expert_ids: int32 [16, 128, 8], P('exp', 'ctx'), may hold values from 0 to 15, all different within a row; in each aligned block of 64 rows (0 to 63, 64 to 127, ..., all dimensions but the last counted through in order) at most 32 rows name the same one
- gate_up: bfloat16 [16, 2048, 768], P('exp'), may hold values from -1 to 1
- down_weight: bfloat16 [16, 384, 2048], P('exp'), may hold values from -0.3125 to 0.3125
Outputs:
- layer_out: bfloat16 [16, 128, 2048], P('exp', 'ctx')
The draws below stay inside these ranges and needn't reach their ends.
Inputs may be any that keep to these rules, and one draw needn't show every extreme that they name: A permutation of 0 to 3; rows b * 32 to b * 32 + 31 of every sequence hold positions span_order[b] * 32 onward. `expert_ids`: each token names 8 different experts; within the 64 rows of one device (aligned blocks of rows) no expert is named by more than 32 tokens.
All inputs are finite; a program needn't handle non-finite values.
Results may differ from the reference program's by a relative error of at most 0.0062.
Values may be sent and summed in bfloat16 or wider, within the bound.
A program may use at most 64 MiB of HBM per device.

```python
import math
import jax
import jax.numpy as jnp
import numpy as np
from jax import lax

D = 2048
H = 16
KVH = 2
HD = 128
GROUP = 8
FFE = 384
TOP = 8
TOK_DEV = 64
HALF = 32
SEQS = 16
LENGTH = 128
SPANS = 4
EXPERTS = 16
CAP = 32


def order_of_spans(key):
    return jax.random.permutation(jax.random.fold_in(key, 11), SPANS).astype(jnp.int32)


def shared_direction(key):
    sign_draw = jax.random.bernoulli(jax.random.fold_in(key, 41), 0.5, (D,))
    return jnp.where(sign_draw, 1.0, -1.0).astype(jnp.float32)


def draw_span_order(key, part):
    return order_of_spans(key)


def draw_residual(key, part):
    array_shape = (SEQS, LENGTH, D)
    direction = shared_direction(key)
    row_sign = jnp.where(jax.random.bernoulli(jax.random.fold_in(key, 43), 0.5, (SEQS, LENGTH, 1)), 1.0, -1.0)
    row_size = jax.random.uniform(jax.random.fold_in(key, 45), (SEQS, LENGTH, 1), jnp.float32, 1.0, 2.0)
    noise = jnp.clip(jax.random.normal(jax.random.fold_in(key, 47), array_shape, jnp.float32), -6.0, 6.0)
    drawn = 0.1 * (noise + row_sign * row_size * direction[None, None, :])
    return drawn.astype(jnp.bfloat16)


def draw_gate_up(key, part):
    array_shape = (EXPERTS, D, 2 * FFE)
    direction = shared_direction(key)
    base = jnp.clip(jax.random.normal(jax.random.fold_in(key, 51), array_shape, jnp.float32), -6.0, 6.0)
    columns = jnp.clip(jax.random.normal(jax.random.fold_in(key, 53), (EXPERTS, 1, 2 * FFE), jnp.float32), -4.0, 4.0)
    drawn = base * D ** (-0.5) + 2.0 / D * direction[None, :, None] * columns
    return drawn.astype(jnp.bfloat16)


def draw_queries(key, part):
    array_shape = (SEQS, LENGTH, H * HD)
    drawn = jnp.clip(jax.random.normal(jax.random.fold_in(key, 21), array_shape, jnp.float32), -6.0, 6.0)
    return drawn.astype(jnp.bfloat16)


def draw_key_rows(key, part):
    array_shape = (SEQS, LENGTH, KVH * HD)
    drawn = jnp.clip(jax.random.normal(jax.random.fold_in(key, 31), array_shape, jnp.float32), -6.0, 6.0)
    return drawn.astype(jnp.bfloat16)


def steps_of(rng, dims, cuts, least, high):
    loudness = 1.0
    for dim, shards_of in cuts:
        draws = jax.random.uniform(jax.random.fold_in(jax.random.fold_in(rng, 6), dim), (shards_of,), jnp.float32, least / len(cuts), high / len(cuts))
        loudness = loudness * jnp.repeat(jnp.exp(draws), dims[dim] // shards_of).reshape((-1,) + (1,) * (len(dims) - 1 - dim))
    return loudness


def routed_block(key, own, number, rows, amount, top, limit, slope):
    ranking = jax.random.permutation(key, amount)
    packed, usual = portions_of(amount, rows * top, limit, slope, True), portions_of(amount, rows * top, limit, slope, False)
    places = jnp.arange(amount)

    def named(tallies, turn):
        used = int((tallies > 0).sum())
        fixed = max(1, used // 4)
        moved = fixed + (places - fixed + turn * (used - fixed)) % max(1, amount - fixed)
        return jnp.zeros((amount,), jnp.int32).at[ranking[jnp.where(places < fixed, places, moved)]].set(jnp.asarray(tallies, jnp.int32))

    tallies = jnp.where(number % 4 == 0, named(packed, number // 4), named(usual, number - number // 4 - 1))
    mixed = jax.random.permutation(jax.random.fold_in(own, 3), amount)
    giver, receiver = mixed[0:amount // 2 * 2:2], mixed[1:amount // 2 * 2:2]
    margin = jnp.minimum(tallies[giver] - 1, limit - tallies[receiver]) // 2
    margin = jnp.where((giver == ranking[0]) | (receiver == ranking[0]) | (tallies[receiver] == 0), 0, jnp.maximum(margin, 0))
    moved = jax.random.randint(jax.random.fold_in(own, 4), (amount // 2,), 0, 1 << 20) % (margin + 1)
    tallies = tallies.at[giver].add(-moved).at[receiver].add(moved)
    items = jnp.searchsorted(jnp.cumsum(tallies), jnp.arange(rows * top), side="right").astype(jnp.int32)
    table = items.reshape(top, rows).T
    table = table[jax.random.permutation(jax.random.fold_in(own, 1), rows)]
    turn = jax.random.randint(jax.random.fold_in(own, 2), (rows, 1), 0, top)
    return jnp.take_along_axis(table, (jnp.arange(top)[None, :] + turn) % top, axis=1)


def portions_of(count, total, reach, lean, full):
    portions = [(1 << 20) // math.isqrt(grade ** lean) + 1 for grade in range(1, count + 1)]
    largest = reach if full else min(reach, max(-(-total // count), total * portions[0] // sum(portions)))
    least = 1 if total - largest >= count - 1 else 0
    counts, surplus = [largest] + [least] * (count - 1), total - largest - least * (count - 1)
    while surplus > 0:
        movable = [i for i in range(1, count) if counts[i] < largest] or [i for i in range(1, count) if counts[i] < reach]
        pool, budget = sum([portions[i] for i in movable]), surplus
        for i in movable:
            addition = min(reach - counts[i], max(1, budget * portions[i] // pool), surplus)
            counts[i] = counts[i] + addition
            surplus = surplus - addition
    return np.array(counts)


def scatter_about(own_key, dims, deviation, most, cuts=(), kind=jnp.bfloat16):
    level = steps_of(own_key, dims, cuts, -0.22, 0.18) if cuts else 1.0
    values = jax.random.normal(own_key, dims, jnp.float32) * deviation * level
    return jnp.minimum(jnp.maximum(values, -most), most).astype(kind)


def setup_inputs(seed: int = 0) -> dict:
    seeds = jax.random.split(jax.random.key(seed), 11)
    residual = draw_residual(jax.random.fold_in(seeds[10], 71), 0)
    queries = draw_queries(jax.random.fold_in(seeds[10], 71), 0)
    key_rows = draw_key_rows(jax.random.fold_in(seeds[10], 71), 0)
    value_rows = scatter_about(seeds[3], (SEQS, LENGTH, KVH * HD), 0.15, 0.8984375, ((0, 16), (1, 2)))
    span_order = draw_span_order(jax.random.fold_in(seeds[10], 71), 0)
    norm_gain = jnp.clip(1.0 + 0.18 * jax.random.normal(seeds[5], (D,), jnp.float32), 0.1, 1.9)
    gate_logits = scatter_about(seeds[6], (SEQS, LENGTH, TOP), 1.5, 6.0, ((0, 16), (1, 2)), jnp.float32)
    expert_ids_keys = jax.random.split(jax.random.fold_in(seeds[7], 1), SEQS * LENGTH // TOK_DEV)
    expert_ids_turns = jax.random.permutation(jax.random.fold_in(seeds[7], 3), SEQS * LENGTH // TOK_DEV)
    expert_ids = jax.vmap(lambda own, number: routed_block(jax.random.fold_in(seeds[7], 2), own, number, TOK_DEV, EXPERTS, TOP, CAP, 1))(expert_ids_keys, expert_ids_turns).reshape((SEQS, LENGTH, TOP))
    gate_up = draw_gate_up(jax.random.fold_in(seeds[10], 71), 0)
    down_weight = scatter_about(seeds[9], (EXPERTS, FFE, D), FFE ** -0.5, 0.3125, ((0, 16),))
    return {"residual": residual, "queries": queries, "key_rows": key_rows, "value_rows": value_rows, "span_order": span_order, "norm_gain": norm_gain, "gate_logits": gate_logits, "expert_ids": expert_ids, "gate_up": gate_up, "down_weight": down_weight}


big_negative = -1e+30
norm_eps = 1e-06

def sequence_positions(span_order):
    row_index = jnp.arange(LENGTH, dtype=jnp.int32)
    return span_order[row_index // HALF].astype(jnp.int32) * HALF + row_index % HALF

def attend_sequence(query_block, key_part, value_part, position):
    query_heads = query_block.astype(jnp.float32).reshape(LENGTH, KVH, GROUP, HD)
    key_heads = key_part.astype(jnp.float32).reshape(LENGTH, KVH, HD)
    value_heads = value_part.astype(jnp.float32).reshape(LENGTH, KVH, HD)
    scores = jnp.einsum('tgqd,cgd->gqtc', query_heads, key_heads, precision=lax.Precision.HIGHEST) * (1.0 / math.sqrt(HD))
    visible = position[None, :] <= position[:, None]
    scores = jnp.where(visible, scores, big_negative)
    largest = lax.optimization_barrier(jnp.max(scores, axis=3, keepdims=True))
    weights = jnp.where(visible, jnp.exp(scores - largest), 0.0)
    accumulated = lax.optimization_barrier(jnp.sum(weights, axis=3))
    rounded = lax.optimization_barrier(weights.astype(jnp.bfloat16)).astype(jnp.float32)
    summed = jnp.einsum('gqtc,cgd->tgqd', rounded, value_heads, precision=lax.Precision.HIGHEST)
    summed = summed / jnp.transpose(accumulated, (2, 0, 1))[..., None]
    return summed.reshape(LENGTH, H * HD).astype(jnp.bfloat16)

def reference(residual, queries, key_rows, value_rows, span_order, norm_gain, gate_logits, expert_ids, gate_up, down_weight):
    position = sequence_positions(span_order)
    attention = lax.map(lambda triple: attend_sequence(triple[0], triple[1], triple[2], position), (queries, key_rows, value_rows))
    attention = lax.optimization_barrier(attention).astype(jnp.float32)
    mixed_rows = residual.astype(jnp.float32).reshape(-1, D) + attention.reshape(-1, D)
    scale_rms = lax.rsqrt(lax.optimization_barrier(jnp.mean(mixed_rows * mixed_rows, axis=1, keepdims=True)) + norm_eps)
    normed = (mixed_rows * scale_rms * norm_gain).astype(jnp.bfloat16)
    logits = gate_logits.reshape(-1, TOP)
    raised = jnp.exp(logits)
    routing_weight = (raised / lax.optimization_barrier(jnp.sum(raised, axis=1, keepdims=True))).reshape(-1)
    flat_experts = expert_ids.reshape(-1).astype(jnp.int32)
    slot_limit = SEQS * LENGTH // TOK_DEV * CAP

    def expert_step(accumulated, inputs):
        expert, weight_pair, weight_down = inputs
        chosen = flat_experts == expert
        picked = jnp.nonzero(chosen, size=slot_limit, fill_value=0)[0].astype(jnp.int32)
        is_live = jnp.arange(slot_limit, dtype=jnp.int32) < jnp.sum(chosen.astype(jnp.int32))
        token_rows = picked // TOP
        rows_in = normed[token_rows]
        projected = jnp.dot(rows_in, weight_pair, preferred_element_type=jnp.float32)
        hidden = (jax.nn.silu(projected[:, :FFE]) * projected[:, FFE:]).astype(jnp.bfloat16)
        result = jnp.dot(hidden, weight_down, preferred_element_type=jnp.float32).astype(jnp.bfloat16)
        result = lax.optimization_barrier(result).astype(jnp.float32)
        factor = jnp.where(is_live, routing_weight[picked], 0.0)
        return (accumulated.at[token_rows].add(result * factor[:, None]), None)
    accumulated = lax.scan(expert_step, jnp.zeros(mixed_rows.shape, jnp.float32), (jnp.arange(EXPERTS, dtype=jnp.int32), gate_up, down_weight))[0]
    return (mixed_rows + accumulated).astype(jnp.bfloat16).reshape(SEQS, LENGTH, D)
```

```python
import functools
import math

import jax
import jax.numpy as jnp
from jax import lax
from jax.experimental import pallas as pl
from jax.experimental.pallas import tpu as pltpu
from jax.sharding import PartitionSpec as P

MESH = pl.DeviceIdType.MESH
HD = 128
big_negative = -1e30
norm_eps = 1e-06
f32 = jnp.float32
bf16 = jnp.bfloat16


def block_positions(span_ref, row_index, rows_per_span):
    which = row_index // rows_per_span
    start = jnp.zeros_like(row_index)
    for b in range(span_ref.shape[0]):
        start = jnp.where(which == b, span_ref[b], start)
    return start * rows_per_span + row_index % rows_per_span


def kernel(
    n, n_ctx,
    residual, queries, key_rows, value_rows, span_order, norm_gain, gate_logits, expert_ids,
    gate_up, down_weight,
    out,
    keys, values, mixed, xg, wg, yb, r1, r2, r3, gu, dw,
    wsem, kv_send, kv_recv, gs, gr, ws, wr, s1, q1, s2, q2, s3, q3u, q3d,
):
    A = n // 4
    tokens = residual.shape[1]
    width = residual.shape[2]
    kvh = key_rows.shape[2] // HD
    group = width // HD // kvh
    me = lax.axis_index("exp")
    ctx = lax.axis_index("ctx")
    c = me % 2
    x = (me // 2) % 2
    z = me // 4

    def idx(zz, xx, cc):
        return (zz * 2 + xx) * 2 + cc

    core_peer = idx(z, x, 1 - c)
    x_peer = idx(z, 1 - x, c)
    up_peer = jnp.minimum(z + 1, A - 1) * 4 + x * 2 + c
    dn_peer = jnp.maximum(z - 1, 0) * 4 + x * 2 + c
    has_up = z < A - 1
    has_dn = z > 0

    gu_copy = pltpu.make_async_copy(gate_up.at[0], gu, wsem.at[0])
    dw_copy = pltpu.make_async_copy(down_weight.at[0], dw, wsem.at[1])
    gu_copy.start()
    dw_copy.start()

    barrier = pltpu.get_barrier_semaphore()
    for k in range(1, n_ctx):
        pl.semaphore_signal(
            barrier, inc=1, device_id={"ctx": (ctx + k) % n_ctx}, device_id_type=MESH
        )
    for peer in (core_peer, x_peer):
        pl.semaphore_signal(barrier, inc=1, device_id={"exp": peer}, device_id_type=MESH)

    @pl.when(has_up)
    def _():
        pl.semaphore_signal(barrier, inc=1, device_id={"exp": up_peer}, device_id_type=MESH)

    @pl.when(has_dn)
    def _():
        pl.semaphore_signal(barrier, inc=1, device_id={"exp": dn_peer}, device_id_type=MESH)

    pl.semaphore_wait(barrier, n_ctx + 1 + jnp.where(has_up, 1, 0) + jnp.where(has_dn, 1, 0))

    def kv_copies(k):
        target = {"ctx": (ctx + k) % n_ctx}
        return [
            pltpu.make_async_remote_copy(
                src.at[0], dst.at[ctx], kv_send.at[i, k], kv_recv.at[i, k],
                device_id=target, device_id_type=MESH,
            )
            for i, (src, dst) in enumerate(((key_rows, keys), (value_rows, values)))
        ]

    for k in range(1, n_ctx):
        for cp in kv_copies(k):
            cp.start()
    keys[ctx] = key_rows[0]
    values[ctx] = value_rows[0]

    raised = jnp.exp(gate_logits[0])
    routing = raised / jnp.sum(raised, axis=1, keepdims=True)
    lanes = lax.broadcasted_iota(jnp.int32, (tokens, 128), 1)
    dense = jnp.zeros((tokens, 128), f32)
    for j in range(routing.shape[1]):
        dense = jnp.where(expert_ids[0][:, j : j + 1] == lanes, routing[:, j : j + 1], dense)
    square = jnp.concatenate([dense, jnp.zeros((128 - tokens, 128), f32)], axis=0)
    wg[me] = jnp.transpose(square)[:n]

    total_keys = n_ctx * tokens
    rows_per_span = total_keys // span_order.shape[0]
    query_pos = block_positions(
        span_order, ctx * tokens + lax.broadcasted_iota(jnp.int32, (tokens, 1), 0), rows_per_span
    )
    key_pos = block_positions(
        span_order, lax.broadcasted_iota(jnp.int32, (1, total_keys), 1), rows_per_span
    )
    visible = jnp.where(key_pos <= query_pos, 1, 0)
    visible = jnp.concatenate([visible] * group, axis=0) > 0

    for k in range(1, n_ctx):
        for cp in kv_copies(k):
            cp.wait()

    for g in range(kvh):
        heads = [g * group + i for i in range(group)]
        q = jnp.concatenate([queries[0, :, h * HD : (h + 1) * HD] for h in heads], axis=0)
        kk = keys[:, :, g * HD : (g + 1) * HD].reshape(total_keys, HD)
        vv = values[:, :, g * HD : (g + 1) * HD].reshape(total_keys, HD)
        scores = lax.dot_general(
            q, kk, (((1,), (1,)), ((), ())), preferred_element_type=f32
        ) * (1.0 / math.sqrt(HD))
        scores = jnp.where(visible, scores, big_negative)
        weights = jnp.where(
            visible, jnp.exp(scores - jnp.max(scores, axis=1, keepdims=True)), 0.0
        )
        total = jnp.sum(weights, axis=1, keepdims=True)
        summed = jnp.dot(weights.astype(bf16), vv, preferred_element_type=f32) / total
        summed = summed.astype(bf16).astype(f32)
        for i, h in enumerate(heads):
            cols = slice(h * HD, (h + 1) * HD)
            mixed[:, cols] = (
                residual[0, :, cols].astype(f32) + summed[i * tokens : (i + 1) * tokens]
            )

    rows = mixed[...]
    scale = lax.rsqrt(jnp.mean(rows * rows, axis=1, keepdims=True) + norm_eps)
    xg[me] = (rows * scale * norm_gain[...]).astype(bf16)

    def relay(slot, target, k):
        return [
            pltpu.make_async_remote_copy(
                buf.at[slot], buf.at[slot], send.at[k], recv.at[slot],
                device_id={"exp": target}, device_id_type=MESH,
            )
            for buf, send, recv in ((xg, gs, gr), (wg, ws, wr))
        ]

    def start(copies):
        for cp in copies:
            cp.start()

    def arrive(slot):
        for cp in relay(slot, core_peer, 0):
            cp.wait_recv()

    up_copy = lambda zz: relay(idx(zz, x, c), up_peer, zz)
    dn_copy = lambda zz: relay(idx(zz, x, c), dn_peer, A + zz)
    x_copy = lambda zz: relay(idx(zz, x, c), x_peer, 2 * A + zz)
    core_copy = lambda zz, xx: relay(idx(zz, xx, c), core_peer, 3 * A + zz * 2 + xx)

    def both(t, body):
        def one(s, carry):
            zz = z + t * (1 - 2 * s)
            ok = (zz >= 0) & (zz < A) & ((t > 0) | (s == 0))

            @pl.when(ok)
            def _():
                body(zz, s)

            return carry

        lax.fori_loop(0, 2, one, 0)

    def own_column(zz, s):
        @pl.when(zz != z)
        def _():
            arrive(idx(zz, x, c))

        @pl.when((zz <= z) & has_up)
        def _():
            start(up_copy(zz))

        @pl.when((zz >= z) & has_dn)
        def _():
            start(dn_copy(zz))

        start(x_copy(zz))
        start(core_copy(zz, x))

    def other_column(zz, s):
        arrive(idx(zz, 1 - x, c))
        start(core_copy(zz, 1 - x))

    def r1_copy(zz, xx):
        return pltpu.make_async_remote_copy(
            yb.at[idx(zz, xx, 1 - c)], r1.at[zz * 2 + xx],
            s1.at[zz * 2 + xx], q1.at[zz * 2 + xx],
            device_id={"exp": core_peer}, device_id_type=MESH,
        )

    def r2_copy(zz):
        return pltpu.make_async_remote_copy(
            yb.at[idx(zz, 1 - x, c)], r2.at[zz], s2.at[zz], q2.at[zz],
            device_id={"exp": x_peer}, device_id_type=MESH,
        )

    def r3_dn(zz):
        return pltpu.make_async_remote_copy(
            yb.at[idx(zz, x, c)], r3.at[zz], s3.at[zz], q3u.at[zz],
            device_id={"exp": dn_peer}, device_id_type=MESH,
        )

    def r3_up(zz):
        return pltpu.make_async_remote_copy(
            yb.at[idx(zz, x, c)], r3.at[zz + 1], s3.at[zz], q3d.at[zz],
            device_id={"exp": up_peer}, device_id_type=MESH,
        )

    units = gate_up.shape[2] // 2

    def expert(zz, s):
        for xx in (0, 1):
            arrive(idx(zz, xx, 1 - c))
        rows_in = xg[pl.ds(zz * 4, 4)].reshape(4 * tokens, width)
        projected = jnp.dot(rows_in, gu[...], preferred_element_type=f32)
        gate = projected[:, :units]
        hidden = (gate / (1.0 + jnp.exp(-gate)) * projected[:, units:]).astype(bf16)
        for j in range(4):
            row = wg[zz * 4 + j, pl.ds(me, 1), :]
            column = jnp.transpose(jnp.broadcast_to(row, (8, 128)))[:tokens, :1]
            result = jnp.dot(
                hidden[j * tokens : (j + 1) * tokens], dw[...], preferred_element_type=f32
            )
            yb[zz * 4 + j] = (result.astype(bf16).astype(f32) * column).astype(bf16)
        for xx in (0, 1):
            r1_copy(zz, xx).start()

    def send_x(zz, s):
        r1_copy(zz, 1 - x).wait_recv()
        slot = idx(zz, 1 - x, c)
        yb[slot] = (yb[slot].astype(f32) + r1[zz * 2 + 1 - x].astype(f32)).astype(bf16)
        r2_copy(zz).start()

    def step(t, carry):
        both(t, own_column)

        @pl.when(t >= 1)
        def _():
            both(t - 1, other_column)

        @pl.when(t >= 2)
        def _():
            @pl.when(t == 2)
            def _():
                gu_copy.wait()
                dw_copy.wait()

            both(t - 2, expert)

        return carry

    lax.fori_loop(0, A, step, 0)
    send_x(z, 0)

    def tail(t, carry):
        @pl.when(t == A)
        def _():
            both(A - 1, other_column)

        both(t - 2, expert)
        return carry

    lax.fori_loop(A, A + 2, tail, 0)

    def scatter_x(i, carry):
        both(A - 1 - i, send_x)
        return carry

    lax.fori_loop(0, A - 1, scatter_x, 0)

    def column_sum(zz):
        r1_copy(zz, x).wait_recv()
        r2_copy(zz).wait_recv()
        return (
            yb[idx(zz, x, c)].astype(f32)
            + r1[zz * 2 + x].astype(f32)
            + r2[zz].astype(f32)
        )

    def send_z(zz, s):
        slot = idx(zz, x, c)
        base = column_sum(zz)

        def pass_on(beyond, copy, landing):
            @pl.when(beyond)
            def _():
                copy(zz).wait_recv()
                yb[slot] = (base + r3[landing].astype(f32)).astype(bf16)

            @pl.when(jnp.logical_not(beyond))
            def _():
                yb[slot] = base.astype(bf16)

            copy(zz).start()

        @pl.when(zz < z)
        def _():
            pass_on(has_up, r3_dn, zz)

        @pl.when(zz > z)
        def _():
            pass_on(has_dn, r3_up, zz + 1)

    def scatter_z(i, carry):
        both(A - 1 - i, send_z)
        return carry

    lax.fori_loop(0, A - 1, scatter_z, 0)

    mixed[...] += column_sum(z)

    @pl.when(has_up)
    def _():
        r3_dn(z).wait_recv()
        mixed[...] += r3[z].astype(f32)

    @pl.when(has_dn)
    def _():
        r3_up(z).wait_recv()
        mixed[...] += r3[z + 1].astype(f32)

    out[0] = mixed[...].astype(bf16)

    def finish(zz, carry):
        def done(copies):
            for cp in copies:
                cp.wait_send()

        @pl.when((zz <= z) & has_up)
        def _():
            done(up_copy(zz))

        @pl.when((zz >= z) & has_dn)
        def _():
            done(dn_copy(zz))

        done(x_copy(zz))
        for xx in (0, 1):
            done(core_copy(zz, xx))
            done([r1_copy(zz, xx)])
        done([r2_copy(zz)])

        @pl.when(zz < z)
        def _():
            done([r3_dn(zz)])

        @pl.when(zz > z)
        def _():
            done([r3_up(zz)])

        return carry

    lax.fori_loop(0, A, finish, 0)


def solution(mesh):
    n = mesh.shape["exp"]
    n_ctx = mesh.shape["ctx"]

    def local(
        residual, queries, key_rows, value_rows, span_order, norm_gain, gate_logits, expert_ids,
        gate_up, down_weight,
    ):
        tokens, width = residual.shape[1], residual.shape[2]
        A = n // 4
        dma = pltpu.SemaphoreType.DMA
        vmem = pl.BlockSpec(memory_space=pltpu.VMEM)
        anywhere = pl.BlockSpec(memory_space=pl.ANY)
        block = lambda count: pltpu.VMEM((count, tokens, width), bf16)
        return pl.pallas_call(
            functools.partial(kernel, n, n_ctx),
            out_shape=jax.ShapeDtypeStruct(residual.shape, bf16),
            in_specs=[vmem] * 4
            + [pl.BlockSpec(memory_space=pltpu.SMEM)]
            + [vmem] * 3
            + [anywhere] * 2,
            out_specs=vmem,
            scratch_shapes=[
                pltpu.VMEM((n_ctx,) + key_rows.shape[1:], bf16),
                pltpu.VMEM((n_ctx,) + value_rows.shape[1:], bf16),
                pltpu.VMEM((tokens, width), f32),
                block(n),
                pltpu.VMEM((n, n, 128), f32),
                block(n),
                block(2 * A),
                block(A),
                block(A + 1),
                pltpu.VMEM(gate_up.shape[1:], bf16),
                pltpu.VMEM(down_weight.shape[1:], bf16),
                dma((2,)),
                dma((2, n_ctx)),
                dma((2, n_ctx)),
                dma((5 * A,)),
                dma((n,)),
                dma((5 * A,)),
                dma((n,)),
                dma((2 * A,)),
                dma((2 * A,)),
                dma((A,)),
                dma((A,)),
                dma((A,)),
                dma((A,)),
                dma((A,)),
            ],
            compiler_params=pltpu.CompilerParams(
                collective_id=0, has_side_effects=True, vmem_limit_bytes=67043328
            ),
        )(
            residual, queries, key_rows, value_rows, span_order, norm_gain[None], gate_logits,
            expert_ids, gate_up, down_weight,
        )

    return jax.shard_map(
        local,
        mesh=mesh,
        in_specs=(
            P("exp", "ctx", None),
            P("exp", "ctx", None),
            P("exp", "ctx", None),
            P("exp", "ctx", None),
            P(),
            P(),
            P("exp", "ctx", None),
            P("exp", "ctx", None),
            P("exp", None, None),
            P("exp", None, None),
        ),
        out_specs=P("exp", "ctx", None),
        check_vma=False,
    )
```

```python
import functools
import math

import jax
import jax.numpy as jnp
from jax import lax
from jax.experimental import pallas as pl
from jax.experimental.pallas import tpu as pltpu
from jax.sharding import PartitionSpec as P

MESH = pl.DeviceIdType.MESH
HD = 128
big_negative = -1e30
norm_eps = 1e-06
f32 = jnp.float32
bf16 = jnp.bfloat16


def block_positions(span_ref, row_index, rows_per_span):
    which = row_index // rows_per_span
    start = jnp.zeros_like(row_index)
    for b in range(span_ref.shape[0]):
        start = jnp.where(which == b, span_ref[b], start)
    return start * rows_per_span + row_index % rows_per_span


def kernel(
    n, n_ctx,
    residual, queries, key_rows, value_rows, span_order, norm_gain, gate_logits, expert_ids,
    gate_up, down_weight,
    out,
    keys, values, mixed, xg, wg, yb, r1, r2, r3, extra, acc, gu, dw,
    wsem, kv_send, kv_recv, gs, gr, ws, wr, s1, q1, s2, q2, s3, q3u, q3d, se, qe,
):
    A = n // 4
    tokens = residual.shape[1]
    width = residual.shape[2]
    kvh = key_rows.shape[2] // HD
    group = width // HD // kvh
    me = lax.axis_index("exp")
    ctx = lax.axis_index("ctx")
    c = me % 2
    x = (me // 2) % 2
    z = me // 4

    def idx(zz, xx, cc):
        return (zz * 2 + xx) * 2 + cc

    core_peer = idx(z, x, 1 - c)
    x_peer = idx(z, 1 - x, c)
    up_peer = jnp.minimum(z + 1, A - 1) * 4 + x * 2 + c
    dn_peer = jnp.maximum(z - 1, 0) * 4 + x * 2 + c
    half = tokens // 2
    pair = z + 1 - 2 * (z % 2)
    pair_peer = idx(pair, x, c)
    detour = (A - 1) * (1 - z % 2)
    pair_detour = (A - 1) * (z % 2)
    has_up = z < A - 1
    has_dn = z > 0

    gu_copy = pltpu.make_async_copy(gate_up.at[0], gu, wsem.at[0])
    dw_copy = pltpu.make_async_copy(down_weight.at[0], dw, wsem.at[1])
    gu_copy.start()
    dw_copy.start()

    barrier = pltpu.get_barrier_semaphore()
    for k in range(1, n_ctx):
        pl.semaphore_signal(
            barrier, inc=1, device_id={"ctx": (ctx + k) % n_ctx}, device_id_type=MESH
        )
    for peer in (core_peer, x_peer):
        pl.semaphore_signal(barrier, inc=1, device_id={"exp": peer}, device_id_type=MESH)

    @pl.when(has_up)
    def _():
        pl.semaphore_signal(barrier, inc=1, device_id={"exp": up_peer}, device_id_type=MESH)

    @pl.when(has_dn)
    def _():
        pl.semaphore_signal(barrier, inc=1, device_id={"exp": dn_peer}, device_id_type=MESH)

    pl.semaphore_wait(barrier, n_ctx + 1 + jnp.where(has_up, 1, 0) + jnp.where(has_dn, 1, 0))

    def kv_copies(k):
        target = {"ctx": (ctx + k) % n_ctx}
        return [
            pltpu.make_async_remote_copy(
                src.at[0], dst.at[ctx], kv_send.at[i, k], kv_recv.at[i, k],
                device_id=target, device_id_type=MESH,
            )
            for i, (src, dst) in enumerate(((key_rows, keys), (value_rows, values)))
        ]

    for k in range(1, n_ctx):
        for cp in kv_copies(k):
            cp.start()
    keys[ctx] = key_rows[0]
    values[ctx] = value_rows[0]

    raised = jnp.exp(gate_logits[0])
    routing = raised / jnp.sum(raised, axis=0, keepdims=True)
    experts = lax.broadcasted_iota(jnp.int32, (n, tokens), 0)
    dense = jnp.zeros((n, tokens), f32)
    for j in range(routing.shape[0]):
        dense = jnp.where(expert_ids[0][j : j + 1] == experts, routing[j : j + 1], dense)
    wg[me] = jnp.zeros((n, 128), f32)
    wg[me, :, :tokens] = dense

    total_keys = n_ctx * tokens
    rows_per_span = total_keys // span_order.shape[0]
    query_pos = block_positions(
        span_order, ctx * tokens + lax.broadcasted_iota(jnp.int32, (tokens, 1), 0), rows_per_span
    )
    key_pos = block_positions(
        span_order, lax.broadcasted_iota(jnp.int32, (1, total_keys), 1), rows_per_span
    )
    visible = jnp.where(key_pos <= query_pos, 1, 0)
    visible = jnp.concatenate([visible] * group, axis=0) > 0

    for k in range(1, n_ctx):
        for cp in kv_copies(k):
            cp.wait()

    for g in range(kvh):
        heads = [g * group + i for i in range(group)]
        q = jnp.concatenate([queries[0, :, h * HD : (h + 1) * HD] for h in heads], axis=0)
        kk = keys[:, :, g * HD : (g + 1) * HD].reshape(total_keys, HD)
        vv = values[:, :, g * HD : (g + 1) * HD].reshape(total_keys, HD)
        scores = lax.dot_general(
            q, kk, (((1,), (1,)), ((), ())), preferred_element_type=f32
        ) * (1.0 / math.sqrt(HD))
        scores = jnp.where(visible, scores, big_negative)
        weights = jnp.where(
            visible, jnp.exp(scores - jnp.max(scores, axis=1, keepdims=True)), 0.0
        )
        total = jnp.sum(weights, axis=1, keepdims=True)
        summed = jnp.dot(weights.astype(bf16), vv, preferred_element_type=f32) / total
        summed = summed.astype(bf16).astype(f32)
        for i, h in enumerate(heads):
            cols = slice(h * HD, (h + 1) * HD)
            mixed[:, cols] = (
                residual[0, :, cols].astype(f32) + summed[i * tokens : (i + 1) * tokens]
            )

    rows = mixed[...]
    scale = lax.rsqrt(jnp.mean(rows * rows, axis=1, keepdims=True) + norm_eps)
    normed = (rows * scale * norm_gain[...]).astype(bf16)
    for h in (0, 1):
        xg[me * 2 + h] = normed[h * half : (h + 1) * half]

    def unit(slot, h, target, k):
        return pltpu.make_async_remote_copy(
            xg.at[slot * 2 + h], xg.at[slot * 2 + h], gs.at[k * 2 + h], gr.at[slot * 2 + h],
            device_id={"exp": target}, device_id_type=MESH,
        )

    def routes(slot, target, k):
        return pltpu.make_async_remote_copy(
            wg.at[slot], wg.at[slot], ws.at[k], wr.at[slot],
            device_id={"exp": target}, device_id_type=MESH,
        )

    def relay(slot, h, target, k):
        unit(slot, h, target, k).start()

        @pl.when(h == 0)
        def _():
            routes(slot, target, k).start()

    def arrive(slot, h):
        unit(slot, h, core_peer, 0).wait_recv()

        @pl.when(h == 0)
        def _():
            routes(slot, core_peer, 0).wait_recv()

    def both(t, body):
        def one(s, carry):
            zz = z + t * (1 - 2 * s)
            ok = (zz >= 0) & (zz < A) & ((t > 0) | (s == 0))

            @pl.when(ok)
            def _():
                body(zz)

            return carry

        lax.fori_loop(0, 2, one, 0)

    def own_column(zz, h):
        slot = idx(zz, x, c)

        @pl.when(zz != z)
        def _():
            arrive(slot, h)

        @pl.when((zz <= z) & has_up)
        def _():
            relay(slot, h, up_peer, zz)

        @pl.when((zz >= z) & has_dn)
        def _():
            relay(slot, h, dn_peer, A + zz)

        @pl.when((zz != detour) | (h == 1))
        def _():
            unit(slot, h, x_peer, 2 * A + zz).start()

        @pl.when(h == 0)
        def _():
            routes(slot, x_peer, 2 * A + zz).start()

        relay(slot, h, core_peer, 3 * A + zz * 2 + x)

    def detour_copy():
        slot = idx(pair_detour, 1 - x, c)
        return pltpu.make_async_remote_copy(
            xg.at[slot * 2], xg.at[slot * 2], se.at[0], gr.at[slot * 2],
            device_id={"exp": pair_peer}, device_id_type=MESH,
        )

    def other_column(zz, h):
        slot = idx(zz, 1 - x, c)
        arrive(slot, h)

        @pl.when((zz == pair_detour) & (h == 0))
        def _():
            detour_copy().start()

        relay(slot, h, core_peer, 3 * A + zz * 2 + 1 - x)

    def r1_copy(zz, xx):
        return pltpu.make_async_remote_copy(
            yb.at[pl.ds(idx(zz, xx, 1 - c) * 2, 2)], r1.at[pl.ds((zz * 2 + xx) * 2, 2)],
            s1.at[zz * 2 + xx], q1.at[zz * 2 + xx],
            device_id={"exp": core_peer}, device_id_type=MESH,
        )

    def r2_copy(zz, h):
        k = zz * 2 + h
        return pltpu.make_async_remote_copy(
            yb.at[idx(zz, 1 - x, c) * 2 + h], r2.at[k], s2.at[k], q2.at[k],
            device_id={"exp": x_peer}, device_id_type=MESH,
        )

    def extra_copy():
        return pltpu.make_async_remote_copy(
            yb.at[idx(detour, 1 - x, c) * 2], extra, se.at[1], qe.at[0],
            device_id={"exp": pair_peer}, device_id_type=MESH,
        )

    def r3_dn(zz, h):
        k = zz * 2 + h
        return pltpu.make_async_remote_copy(
            yb.at[idx(zz, x, c) * 2 + h], r3.at[k], s3.at[k], q3u.at[k],
            device_id={"exp": dn_peer}, device_id_type=MESH,
        )

    def r3_up(zz, h):
        k = zz * 2 + h
        return pltpu.make_async_remote_copy(
            yb.at[idx(zz, x, c) * 2 + h], r3.at[k + 2], s3.at[k], q3d.at[k],
            device_id={"exp": up_peer}, device_id_type=MESH,
        )

    units = gate_up.shape[2] // 2

    def expert(zz, xx):
        for h in (0, 1):
            unit(idx(zz, xx, 1 - c), h, core_peer, 0).wait_recv()
        routes(idx(zz, xx, 1 - c), core_peer, 0).wait_recv()
        first = zz * 4 + xx * 2
        rows_in = xg[pl.ds(first * 2, 4)].reshape(2 * tokens, width)
        projected = jnp.dot(rows_in, gu[...], preferred_element_type=f32)
        gate = projected[:, :units]
        hidden = (gate / (1.0 + jnp.exp(-gate)) * projected[:, units:]).astype(bf16)
        result = jnp.dot(hidden, dw[...], preferred_element_type=f32)
        for j in (0, 1):
            row = wg[first + j, pl.ds(me, 1), :]
            column = jnp.transpose(jnp.broadcast_to(row, (8, 128)))[:tokens, :1]
            scaled = (
                result[j * tokens : (j + 1) * tokens].astype(bf16).astype(f32) * column
            ).astype(bf16)
            for h in (0, 1):
                yb[(first + j) * 2 + h] = scaled[h * half : (h + 1) * half]
        r1_copy(zz, xx).start()

    def send_x(zz, h):
        @pl.when(h == 1)
        def _():
            r1_copy(zz, 1 - x).wait_recv()

        k = idx(zz, 1 - x, c) * 2 + h
        acc[...] = yb[k].astype(f32) + r1[(zz * 2 + 1 - x) * 2 + h].astype(f32)

        @pl.when((zz == pair_detour) & (h == 0))
        def _():
            extra_copy().wait_recv()
            acc[...] += extra[...].astype(f32)

        yb[k] = acc[...].astype(bf16)
        around = (zz == detour) & (h == 0)

        @pl.when(around)
        def _():
            extra_copy().start()

        @pl.when(jnp.logical_not(around))
        def _():
            r2_copy(zz, h).start()

    def step(u, carry):
        t, h = u // 2, u % 2
        both(t, lambda zz: own_column(zz, h))

        @pl.when(u >= 1)
        def _():
            both((u - 1) // 2, lambda zz: other_column(zz, (u - 1) % 2))

        @pl.when(u >= 2)
        def _():
            @pl.when(u == 2)
            def _():
                gu_copy.wait()
                dw_copy.wait()

            both(t - 1, lambda zz: expert(zz, jnp.where(h == 0, x, 1 - x)))

        return carry

    lax.fori_loop(0, 2 * A, step, 0)
    send_x(z, 1)

    def tail(i, carry):
        @pl.when(i == 1)
        def _():
            both(A - 1, lambda zz: other_column(zz, 1))

        both(A - 1, lambda zz: expert(zz, jnp.where(i == 0, x, 1 - x)))
        return carry

    lax.fori_loop(0, 2, tail, 0)

    def scatter_x(i, carry):
        both(A - 1 - i // 2, lambda zz: send_x(zz, 1 - i % 2))
        return carry

    lax.fori_loop(0, 2 * (A - 1), scatter_x, 0)
    send_x(z, 0)

    def column_sum(zz, h):
        @pl.when(h == 1)
        def _():
            r1_copy(zz, x).wait_recv()

        acc[...] = yb[idx(zz, x, c) * 2 + h].astype(f32) + r1[(zz * 2 + x) * 2 + h].astype(f32)

        @pl.when((zz != detour) | (h == 1))
        def _():
            r2_copy(zz, h).wait_recv()
            acc[...] += r2[zz * 2 + h].astype(f32)

        @pl.when((zz <= z) & has_up)
        def _():
            r3_dn(zz, h).wait_recv()
            acc[...] += r3[zz * 2 + h].astype(f32)

        @pl.when((zz >= z) & has_dn)
        def _():
            r3_up(zz, h).wait_recv()
            acc[...] += r3[zz * 2 + 2 + h].astype(f32)

    def send_z(zz, h):
        column_sum(zz, h)
        yb[idx(zz, x, c) * 2 + h] = acc[...].astype(bf16)

        @pl.when(zz < z)
        def _():
            r3_dn(zz, h).start()

        @pl.when(zz > z)
        def _():
            r3_up(zz, h).start()

    def scatter_z(i, carry):
        both(A - 1 - i // 2, lambda zz: send_z(zz, 1 - i % 2))
        return carry

    lax.fori_loop(0, 2 * (A - 1), scatter_z, 0)

    for h in (1, 0):
        column_sum(z, h)
        part = slice(h * half, (h + 1) * half)
        out[0, part] = (mixed[part] + acc[...]).astype(bf16)

    def finish(zz, carry):
        slot = idx(zz, x, c)

        def done(slot, target, k):
            for h in (0, 1):
                unit(slot, h, target, k).wait_send()
            routes(slot, target, k).wait_send()

        @pl.when((zz <= z) & has_up)
        def _():
            done(slot, up_peer, zz)

        @pl.when((zz >= z) & has_dn)
        def _():
            done(slot, dn_peer, A + zz)

        @pl.when(zz != detour)
        def _():
            unit(slot, 0, x_peer, 2 * A + zz).wait_send()
            r2_copy(zz, 0).wait_send()

        unit(slot, 1, x_peer, 2 * A + zz).wait_send()
        r2_copy(zz, 1).wait_send()
        routes(slot, x_peer, 2 * A + zz).wait_send()
        for xx in (0, 1):
            done(idx(zz, xx, c), core_peer, 3 * A + zz * 2 + xx)
            r1_copy(zz, xx).wait_send()

        @pl.when(zz < z)
        def _():
            for h in (0, 1):
                r3_dn(zz, h).wait_send()

        @pl.when(zz > z)
        def _():
            for h in (0, 1):
                r3_up(zz, h).wait_send()

        return carry

    lax.fori_loop(0, A, finish, 0)
    detour_copy().wait_send()
    extra_copy().wait_send()


def solution(mesh):
    n = mesh.shape["exp"]
    n_ctx = mesh.shape["ctx"]

    def local(
        residual, queries, key_rows, value_rows, span_order, norm_gain, gate_logits, expert_ids,
        gate_up, down_weight,
    ):
        tokens, width = residual.shape[1], residual.shape[2]
        A = n // 4
        dma = pltpu.SemaphoreType.DMA
        vmem = pl.BlockSpec(memory_space=pltpu.VMEM)
        anywhere = pl.BlockSpec(memory_space=pl.ANY)
        block = lambda count: pltpu.VMEM((count * 2, tokens // 2, width), bf16)
        return pl.pallas_call(
            functools.partial(kernel, n, n_ctx),
            out_shape=jax.ShapeDtypeStruct(residual.shape, bf16),
            in_specs=[vmem] * 4
            + [pl.BlockSpec(memory_space=pltpu.SMEM)]
            + [vmem] * 3
            + [anywhere] * 2,
            out_specs=vmem,
            scratch_shapes=[
                pltpu.VMEM((n_ctx,) + key_rows.shape[1:], bf16),
                pltpu.VMEM((n_ctx,) + value_rows.shape[1:], bf16),
                pltpu.VMEM((tokens, width), f32),
                block(n),
                pltpu.VMEM((n, n, 128), f32),
                block(n),
                block(2 * A),
                block(A),
                block(A + 1),
                pltpu.VMEM((tokens // 2, width), bf16),
                pltpu.VMEM((tokens // 2, width), f32),
                pltpu.VMEM(gate_up.shape[1:], bf16),
                pltpu.VMEM(down_weight.shape[1:], bf16),
                dma((2,)),
                dma((2, n_ctx)),
                dma((2, n_ctx)),
                dma((10 * A,)),
                dma((2 * n,)),
                dma((5 * A,)),
                dma((n,)),
                dma((2 * A,)),
                dma((2 * A,)),
                dma((2 * A,)),
                dma((2 * A,)),
                dma((2 * A,)),
                dma((2 * A,)),
                dma((2 * A,)),
                dma((2,)),
                dma((1,)),
            ],
            compiler_params=pltpu.CompilerParams(
                collective_id=0, has_side_effects=True, vmem_limit_bytes=67043328
            ),
        )(
            residual, queries, key_rows, value_rows, span_order, norm_gain[None],
            jnp.swapaxes(gate_logits, 1, 2), jnp.swapaxes(expert_ids, 1, 2), gate_up, down_weight,
        )

    return jax.shard_map(
        local,
        mesh=mesh,
        in_specs=(
            P("exp", "ctx", None),
            P("exp", "ctx", None),
            P("exp", "ctx", None),
            P("exp", "ctx", None),
            P(),
            P(),
            P("exp", "ctx", None),
            P("exp", "ctx", None),
            P("exp", None, None),
            P("exp", None, None),
        ),
        out_specs=P("exp", "ctx", None),
        check_vma=False,
    )
```

```python
import functools
import math

import jax
import jax.numpy as jnp
from jax import lax
from jax.experimental import pallas as pl
from jax.experimental.pallas import tpu as pltpu
from jax.sharding import PartitionSpec as P

MESH = pl.DeviceIdType.MESH
HD = 128
big_negative = -1e30
norm_eps = 1e-06
f32 = jnp.float32
bf16 = jnp.bfloat16


def block_positions(span_ref, row_index, rows_per_span):
    which = row_index // rows_per_span
    start = jnp.zeros_like(row_index)
    for b in range(span_ref.shape[0]):
        start = jnp.where(which == b, span_ref[b], start)
    return start * rows_per_span + row_index % rows_per_span


def kernel(
    n, n_ctx,
    residual_in, queries_in, key_rows, value_rows, span_order, norm_gain, gate_logits, expert_ids,
    gate_up, down_weight,
    out,
    residual, queries,
    keys, values, mixed, xg, wg, yb, r1, r2, r3, extra, acc, gu, dw,
    wsem, kv_send, kv_recv, gs, gr, ws, wr, s1, q1, s2, q2, s3, q3u, q3d, se, qe,
):
    A = n // 4
    tokens = residual.shape[1]
    width = residual.shape[2]
    kvh = key_rows.shape[2] // HD
    group = width // HD // kvh
    me = lax.axis_index("exp")
    ctx = lax.axis_index("ctx")
    c = me % 2
    x = (me // 2) % 2
    z = me // 4

    def idx(zz, xx, cc):
        return (zz * 2 + xx) * 2 + cc

    core_peer = idx(z, x, 1 - c)
    x_peer = idx(z, 1 - x, c)
    up_peer = jnp.minimum(z + 1, A - 1) * 4 + x * 2 + c
    dn_peer = jnp.maximum(z - 1, 0) * 4 + x * 2 + c
    half = tokens // 2
    pair = z + 1 - 2 * (z % 2)
    pair_peer = idx(pair, x, c)
    detour = (A - 1) * (1 - z % 2)
    pair_detour = (A - 1) * (z % 2)
    has_up = z < A - 1
    has_dn = z > 0

    barrier = pltpu.get_barrier_semaphore()
    for k in range(1, n_ctx):
        pl.semaphore_signal(
            barrier, inc=1, device_id={"ctx": (ctx + k) % n_ctx}, device_id_type=MESH
        )
    for peer in (core_peer, x_peer):
        pl.semaphore_signal(barrier, inc=1, device_id={"exp": peer}, device_id_type=MESH)

    @pl.when(has_up)
    def _():
        pl.semaphore_signal(barrier, inc=1, device_id={"exp": up_peer}, device_id_type=MESH)

    @pl.when(has_dn)
    def _():
        pl.semaphore_signal(barrier, inc=1, device_id={"exp": dn_peer}, device_id_type=MESH)

    loads = [
        pltpu.make_async_copy(queries_in, queries, wsem.at[0]),
        pltpu.make_async_copy(residual_in, residual, wsem.at[1]),
    ]
    gu_copy = pltpu.make_async_copy(gate_up.at[0], gu, wsem.at[2])
    dw_copy = pltpu.make_async_copy(down_weight.at[0], dw, wsem.at[3])
    for cp in loads:
        cp.start()
    gu_copy.start()
    dw_copy.start()
    pl.semaphore_wait(barrier, n_ctx + 1 + jnp.where(has_up, 1, 0) + jnp.where(has_dn, 1, 0))

    def kv_copies(k):
        target = {"ctx": (ctx + k) % n_ctx}
        return [
            pltpu.make_async_remote_copy(
                src.at[0], dst.at[ctx], kv_send.at[i, k], kv_recv.at[i, k],
                device_id=target, device_id_type=MESH,
            )
            for i, (src, dst) in enumerate(((key_rows, keys), (value_rows, values)))
        ]

    for k in range(1, n_ctx):
        for cp in kv_copies(k):
            cp.start()
    keys[ctx] = key_rows[0]
    values[ctx] = value_rows[0]

    raised = jnp.exp(gate_logits[0])
    routing = raised / jnp.sum(raised, axis=0, keepdims=True)
    experts = lax.broadcasted_iota(jnp.int32, (n, tokens), 0)
    dense = jnp.zeros((n, tokens), f32)
    for j in range(routing.shape[0]):
        dense = jnp.where(expert_ids[0][j : j + 1] == experts, routing[j : j + 1], dense)
    wg[me] = jnp.zeros((n, 128), f32)
    wg[me, :, :tokens] = dense

    total_keys = n_ctx * tokens
    rows_per_span = total_keys // span_order.shape[0]
    query_pos = block_positions(
        span_order, ctx * tokens + lax.broadcasted_iota(jnp.int32, (tokens, 1), 0), rows_per_span
    )
    key_pos = block_positions(
        span_order, lax.broadcasted_iota(jnp.int32, (1, total_keys), 1), rows_per_span
    )
    visible = jnp.where(key_pos <= query_pos, 1, 0)
    visible = jnp.concatenate([visible] * group, axis=0) > 0

    for cp in loads:
        cp.wait()
    for k in range(1, n_ctx):
        for cp in kv_copies(k):
            cp.wait()

    for g in range(kvh):
        heads = [g * group + i for i in range(group)]
        q = jnp.concatenate([queries[0, :, h * HD : (h + 1) * HD] for h in heads], axis=0)
        kk = keys[:, :, g * HD : (g + 1) * HD].reshape(total_keys, HD)
        vv = values[:, :, g * HD : (g + 1) * HD].reshape(total_keys, HD)
        scores = lax.dot_general(
            q, kk, (((1,), (1,)), ((), ())), preferred_element_type=f32
        ) * (1.0 / math.sqrt(HD))
        scores = jnp.where(visible, scores, big_negative)
        weights = jnp.where(
            visible, jnp.exp(scores - jnp.max(scores, axis=1, keepdims=True)), 0.0
        )
        total = jnp.sum(weights, axis=1, keepdims=True)
        summed = jnp.dot(weights.astype(bf16), vv, preferred_element_type=f32) / total
        summed = summed.astype(bf16).astype(f32)
        for i, h in enumerate(heads):
            cols = slice(h * HD, (h + 1) * HD)
            mixed[:, cols] = (
                residual[0, :, cols].astype(f32) + summed[i * tokens : (i + 1) * tokens]
            )

    rows = mixed[...]
    scale = lax.rsqrt(jnp.mean(rows * rows, axis=1, keepdims=True) + norm_eps)
    normed = (rows * scale * norm_gain[...]).astype(bf16)
    for h in (0, 1):
        xg[me * 2 + h] = normed[h * half : (h + 1) * half]

    def unit(slot, h, target, k):
        return pltpu.make_async_remote_copy(
            xg.at[slot * 2 + h], xg.at[slot * 2 + h], gs.at[k * 2 + h], gr.at[slot * 2 + h],
            device_id={"exp": target}, device_id_type=MESH,
        )

    def routes(slot, target, k):
        return pltpu.make_async_remote_copy(
            wg.at[slot], wg.at[slot], ws.at[k], wr.at[slot],
            device_id={"exp": target}, device_id_type=MESH,
        )

    def relay(slot, h, target, k):
        unit(slot, h, target, k).start()

        @pl.when(h == 0)
        def _():
            routes(slot, target, k).start()

    def arrive(slot, h):
        unit(slot, h, core_peer, 0).wait_recv()

        @pl.when(h == 0)
        def _():
            routes(slot, core_peer, 0).wait_recv()

    def both(t, body):
        def one(s, carry):
            zz = z + t * (1 - 2 * s)
            ok = (zz >= 0) & (zz < A) & ((t > 0) | (s == 0))

            @pl.when(ok)
            def _():
                body(zz)

            return carry

        lax.fori_loop(0, 2, one, 0)

    def own_column(zz, h):
        slot = idx(zz, x, c)

        @pl.when(zz != z)
        def _():
            arrive(slot, h)

        @pl.when((zz <= z) & has_up)
        def _():
            relay(slot, h, up_peer, zz)

        @pl.when((zz >= z) & has_dn)
        def _():
            relay(slot, h, dn_peer, A + zz)

        @pl.when((zz != detour) | (h == 1))
        def _():
            unit(slot, h, x_peer, 2 * A + zz).start()

        @pl.when(h == 0)
        def _():
            routes(slot, x_peer, 2 * A + zz).start()

        relay(slot, h, core_peer, 3 * A + zz * 2 + x)

    def detour_copy():
        slot = idx(pair_detour, 1 - x, c)
        return pltpu.make_async_remote_copy(
            xg.at[slot * 2], xg.at[slot * 2], se.at[0], gr.at[slot * 2],
            device_id={"exp": pair_peer}, device_id_type=MESH,
        )

    def other_column(zz, h):
        slot = idx(zz, 1 - x, c)
        arrive(slot, h)

        @pl.when((zz == pair_detour) & (h == 0))
        def _():
            detour_copy().start()

        relay(slot, h, core_peer, 3 * A + zz * 2 + 1 - x)

    def r1_copy(zz, xx):
        return pltpu.make_async_remote_copy(
            yb.at[pl.ds(idx(zz, xx, 1 - c) * 2, 2)], r1.at[pl.ds((zz * 2 + xx) * 2, 2)],
            s1.at[zz * 2 + xx], q1.at[zz * 2 + xx],
            device_id={"exp": core_peer}, device_id_type=MESH,
        )

    def r2_copy(zz, h):
        k = zz * 2 + h
        return pltpu.make_async_remote_copy(
            yb.at[idx(zz, 1 - x, c) * 2 + h], r2.at[k], s2.at[k], q2.at[k],
            device_id={"exp": x_peer}, device_id_type=MESH,
        )

    def extra_copy():
        return pltpu.make_async_remote_copy(
            yb.at[idx(detour, 1 - x, c) * 2], extra, se.at[1], qe.at[0],
            device_id={"exp": pair_peer}, device_id_type=MESH,
        )

    def r3_dn(zz, h):
        k = zz * 2 + h
        return pltpu.make_async_remote_copy(
            yb.at[idx(zz, x, c) * 2 + h], r3.at[k], s3.at[k], q3u.at[k],
            device_id={"exp": dn_peer}, device_id_type=MESH,
        )

    def r3_up(zz, h):
        k = zz * 2 + h
        return pltpu.make_async_remote_copy(
            yb.at[idx(zz, x, c) * 2 + h], r3.at[k + 2], s3.at[k], q3d.at[k],
            device_id={"exp": up_peer}, device_id_type=MESH,
        )

    units = gate_up.shape[2] // 2

    def expert(zz, xx):
        for h in (0, 1):
            unit(idx(zz, xx, 1 - c), h, core_peer, 0).wait_recv()
        routes(idx(zz, xx, 1 - c), core_peer, 0).wait_recv()
        first = zz * 4 + xx * 2
        rows_in = xg[pl.ds(first * 2, 4)].reshape(2 * tokens, width)
        projected = jnp.dot(rows_in, gu[...], preferred_element_type=f32)
        gate = projected[:, :units]
        hidden = (gate / (1.0 + jnp.exp(-gate)) * projected[:, units:]).astype(bf16)
        result = jnp.dot(hidden, dw[...], preferred_element_type=f32)
        for j in (0, 1):
            row = wg[first + j, pl.ds(me, 1), :]
            column = jnp.transpose(jnp.broadcast_to(row, (8, 128)))[:tokens, :1]
            scaled = (
                result[j * tokens : (j + 1) * tokens].astype(bf16).astype(f32) * column
            ).astype(bf16)
            for h in (0, 1):
                yb[(first + j) * 2 + h] = scaled[h * half : (h + 1) * half]
        r1_copy(zz, xx).start()

    def send_x(zz, h):
        @pl.when(h == 1)
        def _():
            r1_copy(zz, 1 - x).wait_recv()

        k = idx(zz, 1 - x, c) * 2 + h
        acc[...] = yb[k].astype(f32) + r1[(zz * 2 + 1 - x) * 2 + h].astype(f32)

        @pl.when((zz == pair_detour) & (h == 0))
        def _():
            extra_copy().wait_recv()
            acc[...] += extra[...].astype(f32)

        yb[k] = acc[...].astype(bf16)
        around = (zz == detour) & (h == 0)

        @pl.when(around)
        def _():
            extra_copy().start()

        @pl.when(jnp.logical_not(around))
        def _():
            r2_copy(zz, h).start()

    def step(u, carry):
        t, h = u // 2, u % 2
        both(t, lambda zz: own_column(zz, h))

        @pl.when(u >= 1)
        def _():
            both((u - 1) // 2, lambda zz: other_column(zz, (u - 1) % 2))

        @pl.when(u >= 2)
        def _():
            @pl.when(u == 2)
            def _():
                gu_copy.wait()
                dw_copy.wait()

            both(t - 1, lambda zz: expert(zz, jnp.where(h == 0, x, 1 - x)))

        return carry

    lax.fori_loop(0, 2 * A, step, 0)
    send_x(z, 1)

    def tail(i, carry):
        @pl.when(i == 1)
        def _():
            both(A - 1, lambda zz: other_column(zz, 1))

        both(A - 1, lambda zz: expert(zz, jnp.where(i == 0, x, 1 - x)))
        return carry

    lax.fori_loop(0, 2, tail, 0)

    def scatter_x(i, carry):
        both(A - 1 - i // 2, lambda zz: send_x(zz, 1 - i % 2))
        return carry

    lax.fori_loop(0, 2 * (A - 1), scatter_x, 0)

    def column_sum(zz, h):
        @pl.when(h == 1)
        def _():
            r1_copy(zz, x).wait_recv()

        acc[...] = yb[idx(zz, x, c) * 2 + h].astype(f32) + r1[(zz * 2 + x) * 2 + h].astype(f32)

        @pl.when((zz != detour) | (h == 1))
        def _():
            r2_copy(zz, h).wait_recv()
            acc[...] += r2[zz * 2 + h].astype(f32)

        @pl.when((zz <= z) & has_up)
        def _():
            r3_dn(zz, h).wait_recv()
            acc[...] += r3[zz * 2 + h].astype(f32)

        @pl.when((zz >= z) & has_dn)
        def _():
            r3_up(zz, h).wait_recv()
            acc[...] += r3[zz * 2 + 2 + h].astype(f32)

    def send_z(zz, h):
        column_sum(zz, h)
        yb[idx(zz, x, c) * 2 + h] = acc[...].astype(bf16)

        @pl.when(zz < z)
        def _():
            r3_dn(zz, h).start()

        @pl.when(zz > z)
        def _():
            r3_up(zz, h).start()

    def scatter_z(i, carry):
        both(A - 1 - i // 2, lambda zz: send_z(zz, 1 - i % 2))
        return carry

    lax.fori_loop(0, A - 1, scatter_z, 0)
    send_x(z, 0)
    lax.fori_loop(A - 1, 2 * (A - 1), scatter_z, 0)

    for h in (1, 0):
        column_sum(z, h)
        part = slice(h * half, (h + 1) * half)
        out[0, part] = (mixed[part] + acc[...]).astype(bf16)

    def finish(zz, carry):
        slot = idx(zz, x, c)

        def done(slot, target, k):
            for h in (0, 1):
                unit(slot, h, target, k).wait_send()
            routes(slot, target, k).wait_send()

        @pl.when((zz <= z) & has_up)
        def _():
            done(slot, up_peer, zz)

        @pl.when((zz >= z) & has_dn)
        def _():
            done(slot, dn_peer, A + zz)

        @pl.when(zz != detour)
        def _():
            unit(slot, 0, x_peer, 2 * A + zz).wait_send()
            r2_copy(zz, 0).wait_send()

        unit(slot, 1, x_peer, 2 * A + zz).wait_send()
        r2_copy(zz, 1).wait_send()
        routes(slot, x_peer, 2 * A + zz).wait_send()
        for xx in (0, 1):
            done(idx(zz, xx, c), core_peer, 3 * A + zz * 2 + xx)
            r1_copy(zz, xx).wait_send()

        @pl.when(zz < z)
        def _():
            for h in (0, 1):
                r3_dn(zz, h).wait_send()

        @pl.when(zz > z)
        def _():
            for h in (0, 1):
                r3_up(zz, h).wait_send()

        return carry

    lax.fori_loop(0, A, finish, 0)
    detour_copy().wait_send()
    extra_copy().wait_send()


def solution(mesh):
    n = mesh.shape["exp"]
    n_ctx = mesh.shape["ctx"]

    def local(
        residual, queries, key_rows, value_rows, span_order, norm_gain, gate_logits, expert_ids,
        gate_up, down_weight,
    ):
        tokens, width = residual.shape[1], residual.shape[2]
        A = n // 4
        dma = pltpu.SemaphoreType.DMA
        vmem = pl.BlockSpec(memory_space=pltpu.VMEM)
        anywhere = pl.BlockSpec(memory_space=pl.ANY)
        block = lambda count: pltpu.VMEM((count * 2, tokens // 2, width), bf16)
        return pl.pallas_call(
            functools.partial(kernel, n, n_ctx),
            out_shape=jax.ShapeDtypeStruct(residual.shape, bf16),
            in_specs=[anywhere] * 2
            + [vmem] * 2
            + [pl.BlockSpec(memory_space=pltpu.SMEM)]
            + [vmem] * 3
            + [anywhere] * 2,
            out_specs=vmem,
            scratch_shapes=[
                pltpu.VMEM(residual.shape, bf16),
                pltpu.VMEM(queries.shape, bf16),
                pltpu.VMEM((n_ctx,) + key_rows.shape[1:], bf16),
                pltpu.VMEM((n_ctx,) + value_rows.shape[1:], bf16),
                pltpu.VMEM((tokens, width), f32),
                block(n),
                pltpu.VMEM((n, n, 128), f32),
                block(n),
                block(2 * A),
                block(A),
                block(A + 1),
                pltpu.VMEM((tokens // 2, width), bf16),
                pltpu.VMEM((tokens // 2, width), f32),
                pltpu.VMEM(gate_up.shape[1:], bf16),
                pltpu.VMEM(down_weight.shape[1:], bf16),
                dma((4,)),
                dma((2, n_ctx)),
                dma((2, n_ctx)),
                dma((10 * A,)),
                dma((2 * n,)),
                dma((5 * A,)),
                dma((n,)),
                dma((2 * A,)),
                dma((2 * A,)),
                dma((2 * A,)),
                dma((2 * A,)),
                dma((2 * A,)),
                dma((2 * A,)),
                dma((2 * A,)),
                dma((2,)),
                dma((1,)),
            ],
            compiler_params=pltpu.CompilerParams(
                collective_id=0, has_side_effects=True, vmem_limit_bytes=67043328
            ),
        )(
            residual, queries, key_rows, value_rows, span_order, norm_gain[None],
            jnp.swapaxes(gate_logits, 1, 2), jnp.swapaxes(expert_ids, 1, 2), gate_up, down_weight,
        )

    return jax.shard_map(
        local,
        mesh=mesh,
        in_specs=(
            P("exp", "ctx", None),
            P("exp", "ctx", None),
            P("exp", "ctx", None),
            P("exp", "ctx", None),
            P(),
            P(),
            P("exp", "ctx", None),
            P("exp", "ctx", None),
            P("exp", None, None),
            P("exp", None, None),
        ),
        out_specs=P("exp", "ctx", None),
        check_vma=False,
    )
```
